256 devices in a mesh: blk: 16 (over z_hi, y), owner: 16 (over z_lo, x, core).
Axes of the slice: x: 4, y: 4, z: 8 (z_hi: 4, z_lo: 2; z = z_hi * 2 + z_lo), core: 2. Of those that a mesh axis runs over, the one named last changes fastest.
Arguments:
- queries: bfloat16 [4096, 16, 4096], P(('blk', 'owner')), may hold values from -6 to 6
- candidates: int32 [4096, 2], P(('blk', 'owner')), may hold values from 0 to 15, all different within a row; in each aligned block of 16 rows (0 to 15, 16 to 31, ...) at most 4 rows name the same one
- train_feat: bfloat16 [16, 1024, 4096], P('owner', 'blk'), may hold values from -0.09375 to 0.09375
- keep_weight: float32 [16, 1024], P('owner', 'blk'), may hold values from 0.1 to 1
Outputs:
- scores: bfloat16 [4096, 2, 16, 1024], P(('blk', 'owner'))
The draws below stay inside these ranges and needn't reach their ends.
Inputs may be any that keep to these rules, and one draw needn't show every extreme that they name: `candidates`: each query block names 2 different training blocks. Within the query blocks of one device (aligned blocks of 16 rows) no training block is named more than 4 times, and some training block is named exactly 4 times.
All inputs are finite; a program needn't handle non-finite values.
Results may differ from the reference program's by a relative error of at most 0.0085.
Values may be sent and summed in bfloat16 or wider, within the bound.
No kernel may reach another device: no remote copies, remote signals or barrier semaphores. Data moves between devices by JAX's collectives and lax.ppermute only.
A program may use at most 128 MiB of HBM per device.

```python
import math
import jax
import jax.numpy as jnp
import numpy as np
from jax import lax

K = 4096
QBR = 16
TBR = 1024
CAND = 2
QB_DEV = 16
NTB = 16
NQB = 4096
MOST = 4


def steps_of(own_key, dims, shards, smallest, high):
    level, own = 1.0, jax.random.fold_in(own_key, 6)
    for axis_at, parts in shards:
        heights = jnp.exp(jax.random.uniform(jax.random.fold_in(own, axis_at), (parts,), jnp.float32, smallest / len(shards), high / len(shards)))
        level = level * jnp.repeat(heights, dims[axis_at] // parts).reshape([-1 if axis == axis_at else 1 for axis in range(len(dims))])
    return level


def routed_block(rng, own, number, rows, count, top, most, lean):
    ranking = jax.random.permutation(rng, count)
    crowded, ordinary = load_shares(count, rows * top, most, lean, True), load_shares(count, rows * top, most, lean, False)
    places = jnp.arange(count)

    def named(sizes, rotation):
        used = int((sizes > 0).sum())
        fixed = max(1, used // 4)
        shifted = fixed + (places - fixed + rotation * (used - fixed)) % max(1, count - fixed)
        return jnp.zeros((count,), jnp.int32).at[ranking[jnp.where(places < fixed, places, shifted)]].set(jnp.asarray(sizes, jnp.int32))

    sizes = jnp.where(number % 4 == 0, named(crowded, number // 4), named(ordinary, number - number // 4 - 1))
    mixed = jax.random.permutation(jax.random.fold_in(own, 3), count)
    giver, taker = mixed[0:count // 2 * 2:2], mixed[1:count // 2 * 2:2]
    room = jnp.minimum(sizes[giver] - 1, most - sizes[taker]) // 2
    room = jnp.where((giver == ranking[0]) | (taker == ranking[0]) | (sizes[taker] == 0), 0, jnp.maximum(room, 0))
    shifted = jax.random.randint(jax.random.fold_in(own, 4), (count // 2,), 0, 1 << 20) % (room + 1)
    sizes = sizes.at[giver].add(-shifted).at[taker].add(shifted)
    labels = jnp.searchsorted(jnp.cumsum(sizes), jnp.arange(rows * top), side="right").astype(jnp.int32)
    grid = labels.reshape(top, rows).T
    grid = grid[jax.random.permutation(jax.random.fold_in(own, 1), rows)]
    rotation = jax.random.randint(jax.random.fold_in(own, 2), (rows, 1), 0, top)
    return jnp.take_along_axis(grid, (jnp.arange(top)[None, :] + rotation) % top, axis=1)


def load_shares(amount, total, bound, skew, full):
    portions = [(1 << 20) // math.isqrt(grade ** skew) + 1 for grade in range(1, amount + 1)]
    largest = bound if full else min(bound, max(-(-total // amount), total * portions[0] // sum(portions)))
    least = 1 if total - largest >= amount - 1 else 0
    holding, spare = [largest] + [least] * (amount - 1), total - largest - least * (amount - 1)
    while spare > 0:
        free = [i for i in range(1, amount) if holding[i] < largest] or [i for i in range(1, amount) if holding[i] < bound]
        whole, left = sum([portions[i] for i in free]), spare
        for i in free:
            addition = min(bound - holding[i], max(1, left * portions[i] // whole), spare)
            holding[i] = holding[i] + addition
            spare = spare - addition
    return np.array(holding)


def gaussian(key, shape, width, reach, pieces=(), held_as=jnp.bfloat16):
    loudness = steps_of(key, shape, pieces, -0.22, 0.18) if pieces else 1.0
    array = jax.random.normal(key, shape, jnp.float32) * width * loudness
    return jnp.minimum(jnp.maximum(array, -reach), reach).astype(held_as)


def setup_inputs(seed: int = 0) -> dict:
    key_of = jax.random.split(jax.random.key(seed), 5)
    queries = gaussian(key_of[0], (NQB, QBR, K), 1.0, 6.0, ((0, 256),))
    candidates_keys = jax.random.split(jax.random.fold_in(key_of[1], 1), NQB // QB_DEV)
    candidates_turns = jax.random.permutation(jax.random.fold_in(key_of[1], 3), NQB // QB_DEV)
    candidates = jax.vmap(lambda own, number: routed_block(jax.random.fold_in(key_of[1], 2), own, number, QB_DEV, NTB, CAND, MOST, 2))(candidates_keys, candidates_turns).reshape((NQB, CAND))
    train_feat = gaussian(key_of[2], (NTB, TBR, K), K ** -0.5, 0.09375, ((0, 16), (1, 16)))
    keep_weight = jnp.clip(0.1 + 0.9 * jax.random.uniform(key_of[3], (NTB, TBR), jnp.float32) ** steps_of(key_of[3], (NTB, TBR), ((0, 16), (1, 16)), -0.2, 0.2), 0.1, 1.0)
    return {"queries": queries, "candidates": candidates, "train_feat": train_feat, "keep_weight": keep_weight}


def reference(queries, candidates, train_feat, keep_weight):
    def one_block(item):
        qblock, cand_row = item
        results = []
        for slot_index in range(CAND):
            target = cand_row[slot_index]
            feats = lax.dynamic_index_in_dim(train_feat, target, 0, keepdims=False)
            weight = lax.dynamic_index_in_dim(keep_weight, target, 0, keepdims=False)
            product = jnp.dot(qblock, feats.T, preferred_element_type=jnp.float32)
            results.append((product * weight[None, :]).astype(jnp.bfloat16))
        return jnp.stack(results, axis=0)

    return lax.map(one_block, (queries, candidates))
```

```python
import functools

import jax
import jax.numpy as jnp
from jax import lax
from jax.experimental import pallas as pl
from jax.experimental.pallas import tpu as pltpu
from jax.sharding import PartitionSpec as P


ZH, Y, ZL, X, C = 4, 4, 2, 4, 2
Z = ZH * ZL
BOTH = ("blk", "owner")
MOST = 4
SOURCES = X * C
PIECES = Y * Z


def flat(y, z, x, c):
    return ((z // ZL) * Y + y) * (ZL * X * C) + (z % ZL) * X * C + x * C + c


def permute(a, to):
    pairs = [
        (flat(y, z, x, c), flat(*to(y, z, x, c)))
        for z in range(Z)
        for y in range(Y)
        for x in range(X)
        for c in range(C)
    ]
    return lax.ppermute(a, BOTH, pairs)


def move_x(a, step):
    return permute(a, lambda y, z, x, c: (y, z, (x + step) % X, c))


def move_y(a, step):
    return permute(a, lambda y, z, x, c: ((y + step) % Y, z, x, c))


def move_z(a, step):
    return permute(a, lambda y, z, x, c: (y, (z + step) % Z, x, c))


def swap_core(a):
    return permute(a, lambda y, z, x, c: (y, z, x, c ^ 1))


def doubled(a, bit, to):
    other = permute(a, to)
    return jnp.where(bit == 0, jnp.stack([a, other]), jnp.stack([other, a]))


def score_kernel(table, sources, places, weight, *refs):
    pieces, queries = refs[:PIECES], refs[PIECES : PIECES + 10]
    outs = refs[PIECES + 10 : PIECES + 10 + SOURCES]
    feats, picked, scores, counts, piece_sem, pick_sem, out_sem = refs[PIECES + 10 + SOURCES :]
    cap = SOURCES * MOST
    for i in range(PIECES):
        pltpu.make_async_copy(pieces[i], feats.at[places[i]], piece_sem.at[i]).start()

    def each_slot(tb, visit):
        count = jnp.int32(0)
        for s in range(SOURCES):
            for r in range(MOST):
                block = table[tb, sources[s], r]
                visit(s, r, block, count)
                count = count + jnp.where(block >= 0, 1, 0)
        return count

    def fetch(tb, s, r, block, count):
        dx, dc = s // C, s % C
        slot = tb * cap + count

        def go(ref, index):
            pltpu.make_async_copy(ref.at[index], picked.at[slot], pick_sem.at[slot]).start()

        if dx == 2:
            low, high = queries[5 * dc + 3], queries[5 * dc + 4]
            half = low.shape[0]

            @pl.when((block >= 0) & (block < half))
            def _():
                go(low, block)

            @pl.when(block >= half)
            def _():
                go(high, block - half)
        else:
            ref = queries[5 * dc + {0: 0, 1: 1, 3: 2}[dx]]

            @pl.when(block >= 0)
            def _():
                go(ref, block)

    for tb in range(ZL):
        counts[tb] = each_slot(tb, functools.partial(fetch, tb))
    for i in range(PIECES):
        pltpu.make_async_copy(pieces[i], feats.at[places[i]], piece_sem.at[i]).wait()
    group = 16
    wide = 4
    tiles = PIECES // ZL // wide
    rows = picked.shape[1]
    depth = picked.shape[2]
    cols = wide * feats.shape[1]

    @pl.loop(0, ZL)
    def _(tb):
        @pl.loop(0, counts[tb])
        def _(p):
            slot = tb * cap + p
            pltpu.make_async_copy(
                queries[0].at[0], picked.at[slot], pick_sem.at[slot]
            ).wait()

        @pl.loop(0, (counts[tb] + group - 1) // group)
        def _(m):
            start = tb * cap + m * group

            @pl.loop(0, tiles)
            def _(n):
                q = picked[pl.ds(start, group)].reshape(group * rows, depth)
                f = feats[pl.ds((tb * tiles + n) * wide, wide)].reshape(cols, depth)
                product = lax.dot_general(
                    q, f, (((1,), (1,)), ((), ())), preferred_element_type=jnp.float32
                )
                scaled = (product * weight[tb * tiles + n]).astype(jnp.bfloat16)
                at = pl.ds(pl.multiple_of(n * cols, cols), cols)
                scores[pl.ds(start, group), :, at] = scaled.reshape(group, rows, cols)

    for tb in range(ZL):

        def give(s, r, block, count, tb=tb):
            @pl.when(block >= 0)
            def _():
                pltpu.make_async_copy(
                    scores.at[tb * cap + count],
                    outs[s].at[tb * MOST + r],
                    out_sem.at[tb * cap + count],
                ).start()

        each_slot(tb, give)

    @pl.loop(0, ZL)
    def _(tb):
        @pl.loop(0, counts[tb])
        def _(p):
            slot = tb * cap + p
            pltpu.make_async_copy(scores.at[slot], outs[0].at[0], out_sem.at[slot]).wait()


def place_kernel(select, *refs):
    returned, out, held, in_sem, out_sem = refs[:SOURCES], *refs[SOURCES:]
    size = returned[0].shape[0]
    for s in range(SOURCES):
        pltpu.make_async_copy(
            returned[s], held.at[pl.ds(s * size, size)], in_sem.at[s]
        ).start()
    for s in range(SOURCES):
        pltpu.make_async_copy(
            returned[s], held.at[pl.ds(s * size, size)], in_sem.at[s]
        ).wait()
    for p in range(out.shape[0]):
        pltpu.make_async_copy(held.at[select[p]], out.at[p], out_sem.at[p]).start()
    for p in range(out.shape[0]):
        pltpu.make_async_copy(held.at[select[p]], out.at[p], out_sem.at[p]).wait()


def local(queries, candidates, train_feat, keep_weight):
    blocks, rows, depth = queries.shape
    cands = candidates.shape[1]
    piece_rows = train_feat.shape[1]
    pairs = blocks * cands
    blk, owner = lax.axis_index("blk"), lax.axis_index("owner")
    zh, y = blk // Y, blk % Y
    zl, x, c = owner // (X * C), owner // C % X, owner % C
    z = zh * ZL + zl

    before = move_x(queries, 1)
    after = move_x(queries, -1)
    far_low = move_x(before[: blocks // 2], 1)
    far_high = move_x(after[blocks // 2 :], -1)
    mine = [queries, before, after, far_low, far_high]
    ring = mine + [swap_core(a) for a in mine]

    own = train_feat[0]
    pieces = {(0, 0): own}
    pieces[1, 0] = move_y(own, 1)
    for k in range(1, 4):
        for dy in (0, 1):
            pieces[dy, k] = move_z(pieces[dy, k - 1], 1)
            pieces[dy, -k % Z] = move_z(pieces[dy, (1 - k) % Z], -1)
    pieces[0, 4] = move_z(pieces[0, 3], 1)
    pieces[1, 4] = move_z(pieces[1, 5], -1)
    for k in range(Z):
        pieces[3, k] = move_y(pieces[0, k], -1)
        if k != 5:
            pieces[2, k] = move_y(pieces[1, k], 1)
    pieces[2, 5] = move_z(pieces[2, 6], -1)
    keys = sorted(pieces)
    places = jnp.stack(
        [
            ((z - dz) % Z % ZL) * (ZH * Y) + ((z - dz) % Z // ZL) * Y + (y - dy) % Y
            for dy, dz in keys
        ]
    ).astype(jnp.int32)

    w = keep_weight[0]
    w = doubled(w, y & 1, lambda y, z, x, c: (y ^ 1, z, x, c))
    w = doubled(w, y >> 1, lambda y, z, x, c: (y ^ 2, z, x, c))
    w = doubled(w, zl, lambda y, z, x, c: (y, z ^ 1, x, c))
    w = doubled(w, zh & 1, lambda y, z, x, c: (y, z ^ 2, x, c))
    w = doubled(w, zh >> 1, lambda y, z, x, c: (y, z ^ 4, x, c))
    weight = w.reshape(ZH, ZL, Y * piece_rows).transpose(1, 0, 2).reshape(-1, 1, 4 * piece_rows)
    targets = candidates.reshape(pairs)
    named = doubled(targets, c, lambda y, z, x, c: (y, z, x, c ^ 1))
    named = doubled(named, x & 1, lambda y, z, x, c: (y, z, x ^ 1, c))
    named = doubled(named, x >> 1, lambda y, z, x, c: (y, z, x ^ 2, c))
    named = named.reshape(SOURCES, pairs)

    earlier = (jnp.arange(pairs)[:, None] < jnp.arange(pairs)[None, :]).astype(jnp.float32)
    held = jnp.arange(ZL) * (X * C) + x * C + c
    hot = (named[None] == held[:, None, None]).astype(jnp.float32)
    rank = jnp.dot(hot.reshape(-1, pairs), earlier).reshape(hot.shape)
    chosen = hot[:, :, None, :] * (
        rank[:, :, None, :] == jnp.arange(MOST, dtype=jnp.float32)[None, None, :, None]
    )
    block_of = (jnp.arange(pairs) // cands + 1).astype(jnp.float32)
    table = jnp.sum(chosen * block_of, axis=3).astype(jnp.int32) - 1
    sources = jnp.stack(
        [(x - dx) % X * C + (c ^ dc) for dx in range(X) for dc in range(C)]
    ).astype(jnp.int32)

    target_hot = (targets[None, :] == jnp.arange(ZL * X * C)[:, None]).astype(jnp.float32)
    my_rank = jnp.sum(jnp.dot(target_hot, earlier) * target_hot, axis=0).astype(jnp.int32)
    from_x, from_c = targets // C % X, targets % C
    from_index = (from_x - x) % X * C + (from_c ^ c)
    select = (from_index * ZL + targets // (X * C)) * MOST + my_rank

    smem = pl.BlockSpec(memory_space=pltpu.SMEM)
    vmem = pl.BlockSpec(memory_space=pltpu.VMEM)
    anywhere = pl.BlockSpec(memory_space=pl.ANY)
    cap = SOURCES * MOST
    train_rows = ZH * Y * piece_rows
    scored = pl.pallas_call(
        score_kernel,
        out_shape=[
            jax.ShapeDtypeStruct((ZL * MOST, rows, train_rows), jnp.bfloat16)
        ] * SOURCES,
        in_specs=[smem] * 3 + [vmem] + [anywhere] * (PIECES + 10),
        out_specs=[anywhere] * SOURCES,
        scratch_shapes=[
            pltpu.VMEM((PIECES, piece_rows, depth), jnp.bfloat16),
            pltpu.VMEM((ZL * cap, rows, depth), jnp.bfloat16),
            pltpu.VMEM((ZL * cap, rows, train_rows), jnp.bfloat16),
            pltpu.SMEM((ZL,), jnp.int32),
            pltpu.SemaphoreType.DMA((PIECES,)),
            pltpu.SemaphoreType.DMA((ZL * cap,)),
            pltpu.SemaphoreType.DMA((ZL * cap,)),
        ],
        cost_estimate=pl.CostEstimate(
            flops=2 * pairs * rows * train_rows * depth,
            bytes_accessed=24 << 20,
            transcendentals=0,
        ),
        name="score",
    )(table, sources, places, weight, *[pieces[k] for k in keys], *ring)

    returned = []
    for s in range(SOURCES):
        dx, dc = s // C, s % C
        if s == 0:
            returned.append(scored[0])
        else:
            returned.append(
                permute(
                    scored[s],
                    lambda y, z, x, c, dx=dx, dc=dc: (y, z, (x - dx) % X, c ^ dc),
                )
            )
    out = pl.pallas_call(
        place_kernel,
        out_shape=jax.ShapeDtypeStruct((pairs, rows, train_rows), jnp.bfloat16),
        in_specs=[smem] + [anywhere] * SOURCES,
        out_specs=anywhere,
        scratch_shapes=[
            pltpu.VMEM((SOURCES * ZL * MOST, rows, train_rows), jnp.bfloat16),
            pltpu.SemaphoreType.DMA((SOURCES,)),
            pltpu.SemaphoreType.DMA((pairs,)),
        ],
        name="place",
    )(select, *returned)
    return out.reshape(blocks, cands, rows, train_rows)


def solution(mesh):
    return jax.shard_map(
        local,
        mesh=mesh,
        in_specs=(
            P(("blk", "owner"), None, None),
            P(("blk", "owner"), None),
            P("owner", "blk", None),
            P("owner", "blk"),
        ),
        out_specs=P(("blk", "owner"), None, None, None),
        check_vma=False,
    )
```

```python
import functools

import jax
import jax.numpy as jnp
from jax import lax
from jax.experimental import pallas as pl
from jax.experimental.pallas import tpu as pltpu
from jax.sharding import PartitionSpec as P


ZH, Y, ZL, X, C = 4, 4, 2, 4, 2
Z = ZH * ZL
BOTH = ("blk", "owner")
MOST = 4
SOURCES = X * C


EARLY, LATE = (0, 1, 7, 2, 6), (3, 5, 4)


def flat(y, z, x, c):
    return ((z // ZL) * Y + y) * (ZL * X * C) + (z % ZL) * X * C + x * C + c


def permute(a, to):
    pairs = [
        (flat(y, z, x, c), flat(*to(y, z, x, c)))
        for z in range(Z)
        for y in range(Y)
        for x in range(X)
        for c in range(C)
    ]
    return lax.ppermute(a, BOTH, pairs)


def move_x(a, step):
    return permute(a, lambda y, z, x, c: (y, z, (x + step) % X, c))


def move_y(a, step):
    return permute(a, lambda y, z, x, c: ((y + step) % Y, z, x, c))


def move_z(a, step):
    return permute(a, lambda y, z, x, c: (y, (z + step) % Z, x, c))


def swap_core(a):
    return permute(a, lambda y, z, x, c: (y, z, x, c ^ 1))


def doubled(a, bit, to):
    other = permute(a, to)
    return jnp.where(bit == 0, jnp.stack([a, other]), jnp.stack([other, a]))


def score_kernel(groups, table, sources, places, weight_at, weight, *refs):
    count_q = 5 * C
    pieces, queries = refs[: groups * Y], refs[groups * Y : groups * Y + count_q]
    outs = refs[groups * Y + count_q : groups * Y + count_q + SOURCES]
    feats, picked, scores, counts, first, piece_sem, pick_sem, out_sem = refs[
        groups * Y + count_q + SOURCES :
    ]
    cap = SOURCES * MOST
    for g in range(groups):
        for dy in range(Y):
            pltpu.make_async_copy(
                pieces[g * Y + dy], feats.at[g * Y + places[dy]], piece_sem.at[g * Y + dy]
            ).start()

    def fetch(slot, s, block):
        dx, dc = s // C, s % C

        def go(ref, index):
            pltpu.make_async_copy(ref.at[index], picked.at[slot], pick_sem.at[slot]).start()

        if dx == 2:
            low, high = queries[5 * dc + 3], queries[5 * dc + 4]
            half = low.shape[0]

            @pl.when((block >= 0) & (block < half))
            def _():
                go(low, block)

            @pl.when(block >= half)
            def _():
                go(high, block - half)
        else:
            ref = queries[5 * dc + {0: 0, 1: 1, 3: 2}[dx]]

            @pl.when(block >= 0)
            def _():
                go(ref, block)

    for tb in range(ZL):
        count = jnp.int32(0)
        for s in range(SOURCES):
            first[tb, s] = count
            for r in range(MOST):
                block = table[tb, sources[s], r]
                fetch(tb * cap + count, s, block)
                count = count + jnp.where(block >= 0, 1, 0)
        counts[tb] = count

    @pl.loop(0, ZL)
    def _(tb):
        @pl.loop(0, counts[tb])
        def _(p):
            slot = tb * cap + p
            pltpu.make_async_copy(
                queries[0].at[0], picked.at[slot], pick_sem.at[slot]
            ).wait()

    group = 16
    rows, depth = picked.shape[1:]
    cols = Y * feats.shape[1]

    @pl.loop(0, groups)
    def _(g):
        for dy in range(Y):
            pltpu.make_async_copy(
                pieces[0], feats.at[g * Y], piece_sem.at[g * Y + dy]
            ).wait()
        tb = weight_at[g] // ZH

        @pl.loop(0, (counts[tb] + group - 1) // group)
        def _(m):
            q = picked[pl.ds(tb * cap + m * group, group)].reshape(group * rows, depth)
            f = feats[pl.ds(g * Y, Y)].reshape(cols, depth)
            product = lax.dot_general(
                q, f, (((1,), (1,)), ((), ())), preferred_element_type=jnp.float32
            )
            scaled = (product * weight[weight_at[g]]).astype(jnp.bfloat16)
            scores[g, pl.ds(m * group, group)] = scaled.reshape(group, rows, cols)

        for s in range(SOURCES):
            pltpu.make_async_copy(
                scores.at[g, pl.ds(first[tb, s], MOST)],
                outs[s].at[g],
                out_sem.at[g * SOURCES + s],
            ).start()

    @pl.loop(0, groups * SOURCES)
    def _(i):
        pltpu.make_async_copy(
            scores.at[0, pl.ds(0, MOST)], outs[0].at[0], out_sem.at[i]
        ).wait()


def score(groups, table, sources, places, weight_at, weight, pieces, ring):
    rows, depth = ring[0].shape[1:]
    piece_rows = pieces[0].shape[0]
    cols = Y * piece_rows
    cap = SOURCES * MOST
    smem = pl.BlockSpec(memory_space=pltpu.SMEM)
    anywhere = pl.BlockSpec(memory_space=pltpu.HBM)
    return pl.pallas_call(
        functools.partial(score_kernel, groups),
        out_shape=[jax.ShapeDtypeStruct((groups, MOST, rows, cols), jnp.bfloat16)] * SOURCES,
        in_specs=[smem] * 4
        + [pl.BlockSpec(memory_space=pltpu.VMEM)]
        + [anywhere] * (len(pieces) + len(ring)),
        out_specs=[anywhere] * SOURCES,
        scratch_shapes=[
            pltpu.VMEM((groups * Y, piece_rows, depth), jnp.bfloat16),
            pltpu.VMEM((ZL * cap, rows, depth), jnp.bfloat16),
            pltpu.VMEM((groups, cap + MOST, rows, cols), jnp.bfloat16),
            pltpu.SMEM((ZL,), jnp.int32),
            pltpu.SMEM((ZL, SOURCES), jnp.int32),
            pltpu.SemaphoreType.DMA((groups * Y,)),
            pltpu.SemaphoreType.DMA((ZL * cap,)),
            pltpu.SemaphoreType.DMA((groups * SOURCES,)),
        ],
        cost_estimate=pl.CostEstimate(
            flops=2 * groups * cap * rows * cols * depth,
            bytes_accessed=groups * cols * depth * 2 + (8 << 20),
            transcendentals=0,
        ),
    )(table, sources, places, weight_at, weight, *pieces, *ring)


def place_kernel(select, *refs):
    early, late = refs[:SOURCES], refs[SOURCES : 2 * SOURCES]
    out, held, in_sem = refs[2 * SOURCES :]
    copies = []
    for s in range(SOURCES):
        at = 0
        for part, ref in enumerate((early[s], late[s])):
            copies.append(
                pltpu.make_async_copy(
                    ref, held.at[pl.ds(at, ref.shape[0]), s], in_sem.at[part * SOURCES + s]
                )
            )
            at += ref.shape[0]
    for copy in copies:
        copy.start()
    for copy in copies:
        copy.wait()
    cols = held.shape[-1]

    @pl.loop(0, out.shape[0])
    def _(p):
        for h in range(ZH):
            code = select[p * ZH + h]
            out[p, :, h * cols : (h + 1) * cols] = held[
                code // (SOURCES * MOST), code // MOST % SOURCES, code % MOST
            ]


def local(queries, candidates, train_feat, keep_weight):
    blocks, rows, _ = queries.shape
    cands = candidates.shape[1]
    piece_rows = train_feat.shape[1]
    pairs = blocks * cands
    blk, owner = lax.axis_index("blk"), lax.axis_index("owner")
    zh, y = blk // Y, blk % Y
    zl, x, c = owner // (X * C), owner // C % X, owner % C
    z = zh * ZL + zl

    before = move_x(queries, 1)
    after = move_x(queries, -1)
    far_low = move_x(before[: blocks // 2], 1)
    far_high = move_x(after[blocks // 2 :], -1)
    mine = [queries, before, after, far_low, far_high]
    ring = mine + [swap_core(a) for a in mine]

    own = train_feat[0]
    pieces = {(0, 0): own}
    pieces[1, 0] = move_y(own, 1)
    for k in range(1, 4):
        for dy in (0, 1):
            pieces[dy, k] = move_z(pieces[dy, k - 1], 1)
            pieces[dy, Z - k] = move_z(pieces[dy, (Z - k + 1) % Z], -1)
    pieces[0, 4] = move_z(pieces[0, 3], 1)
    pieces[1, 4] = move_z(pieces[1, 5], -1)
    for k in range(Z):
        pieces[3, k] = move_y(pieces[0, k], -1)
        if k != 5:
            pieces[2, k] = move_y(pieces[1, k], 1)
    pieces[2, 5] = move_z(pieces[2, 6], -1)
    places = jnp.stack([(y - dy) % Y for dy in range(Y)]).astype(jnp.int32)

    w = keep_weight[0]
    w = doubled(w, y & 1, lambda y, z, x, c: (y ^ 1, z, x, c))
    w = doubled(w, y >> 1, lambda y, z, x, c: (y ^ 2, z, x, c))
    w = doubled(w, zl, lambda y, z, x, c: (y, z ^ 1, x, c))
    w = doubled(w, zh & 1, lambda y, z, x, c: (y, z ^ 2, x, c))
    w = doubled(w, zh >> 1, lambda y, z, x, c: (y, z ^ 4, x, c))
    weight = w.reshape(ZH, ZL, Y * piece_rows).transpose(1, 0, 2).reshape(-1, 1, 4 * piece_rows)
    targets = candidates.reshape(pairs)
    named = doubled(targets, c, lambda y, z, x, c: (y, z, x, c ^ 1))
    named = doubled(named, x & 1, lambda y, z, x, c: (y, z, x ^ 1, c))
    named = doubled(named, x >> 1, lambda y, z, x, c: (y, z, x ^ 2, c))
    named = named.reshape(SOURCES, pairs)

    earlier = (jnp.arange(pairs)[:, None] < jnp.arange(pairs)[None, :]).astype(jnp.float32)
    held = jnp.arange(ZL) * (X * C) + x * C + c
    hot = (named[None] == held[:, None, None]).astype(jnp.float32)
    rank = jnp.dot(hot.reshape(-1, pairs), earlier).reshape(hot.shape)
    chosen = hot[:, :, None, :] * (
        rank[:, :, None, :] == jnp.arange(MOST, dtype=jnp.float32)[None, None, :, None]
    )
    block_of = (jnp.arange(pairs) // cands + 1).astype(jnp.float32)
    table = jnp.sum(chosen * block_of, axis=3).astype(jnp.int32) - 1
    sources = jnp.stack(
        [(x - dx) % X * C + (c ^ dc) for dx in range(X) for dc in range(C)]
    ).astype(jnp.int32)

    target_hot = (targets[None, :] == jnp.arange(ZL * X * C)[:, None]).astype(jnp.float32)
    my_rank = jnp.sum(jnp.dot(target_hot, earlier) * target_hot, axis=0).astype(jnp.int32)
    from_x, from_c = targets // C % X, targets % C
    from_index = (from_x - x) % X * C + (from_c ^ c)
    order = EARLY + LATE
    row_of = jnp.array([order.index(dz) for dz in range(Z)], jnp.int32)
    away = (z - (jnp.arange(ZH)[None, :] * ZL + targets[:, None] // (X * C))) % Z
    row = jnp.sum(
        jnp.where(away[:, :, None] == jnp.arange(Z)[None, None, :], row_of[None, None, :], 0),
        axis=2,
    )
    select = ((row * SOURCES + from_index[:, None]) * MOST + my_rank[:, None]).reshape(-1)

    returned = []
    for steps in (EARLY, LATE):
        weight_at = jnp.stack(
            [(z - dz) % Z % ZL * ZH + (z - dz) % Z // ZL for dz in steps]
        ).astype(jnp.int32)
        scored = score(
            len(steps),
            table,
            sources,
            places,
            weight_at,
            weight,
            [pieces[dy, dz] for dz in steps for dy in range(Y)],
            ring,
        )
        for s in range(SOURCES):
            dx, dc = s // C, s % C
            if s == 0:
                returned.append(scored[0])
            else:
                returned.append(
                    permute(
                        scored[s], lambda y, z, x, c, dx=dx, dc=dc: (y, z, (x - dx) % X, c ^ dc)
                    )
                )
    out = pl.pallas_call(
        place_kernel,
        out_shape=jax.ShapeDtypeStruct((pairs, rows, Z * Y * piece_rows // ZL), jnp.bfloat16),
        in_specs=[pl.BlockSpec(memory_space=pltpu.SMEM)]
        + [pl.BlockSpec(memory_space=pltpu.VMEM)] * len(returned),
        out_specs=pl.BlockSpec(memory_space=pltpu.VMEM),
        scratch_shapes=[
            pltpu.VMEM((Z, SOURCES, MOST, rows, Y * piece_rows), jnp.bfloat16),
            pltpu.SemaphoreType.DMA((len(returned),)),
        ],
        name="place",
    )(select, *returned)
    return out.reshape(blocks, cands, rows, -1)


def solution(mesh):
    return jax.shard_map(
        local,
        mesh=mesh,
        in_specs=(
            P(("blk", "owner"), None, None),
            P(("blk", "owner"), None),
            P("owner", "blk", None),
            P("owner", "blk"),
        ),
        out_specs=P(("blk", "owner"), None, None, None),
        check_vma=False,
    )
```

```python
import functools

import jax
import jax.numpy as jnp
from jax import lax
from jax.experimental import pallas as pl
from jax.experimental.pallas import tpu as pltpu
from jax.sharding import PartitionSpec as P


ZH, Y, ZL, X, C = 4, 4, 2, 4, 2
Z = ZH * ZL
BOTH = ("blk", "owner")
MOST = 4
SOURCES = X * C


EARLY, LATE = (0, 1, 7, 2, 6), (3, 5, 4)


def flat(y, z, x, c):
    return ((z // ZL) * Y + y) * (ZL * X * C) + (z % ZL) * X * C + x * C + c


def permute(a, to):
    pairs = [
        (flat(y, z, x, c), flat(*to(y, z, x, c)))
        for z in range(Z)
        for y in range(Y)
        for x in range(X)
        for c in range(C)
    ]
    return lax.ppermute(a, BOTH, pairs)


def move_y(a, step):
    return permute(a, lambda y, z, x, c: ((y + step) % Y, z, x, c))


def move_z(a, step):
    return permute(a, lambda y, z, x, c: (y, (z + step) % Z, x, c))


def swap_core(a):
    return permute(a, lambda y, z, x, c: (y, z, x, c ^ 1))


def doubled(a, bit, to):
    other = permute(a, to)
    return jnp.where(bit == 0, jnp.stack([a, other]), jnp.stack([other, a]))


def score_kernel(groups, where, table, sources, places, block_of, *refs):
    held = max(i for i, _ in where) + 1
    pieces, queries = refs[:held], refs[held : held + SOURCES]
    outs = refs[held + SOURCES : held + 2 * SOURCES]
    feats, picked, scores, counts, first, piece_sem, pick_sem, out_sem = refs[
        held + 2 * SOURCES :
    ]
    cap = SOURCES * MOST
    for g in range(groups):
        for dy in range(Y):
            i, half = where[g * Y + dy]
            pltpu.make_async_copy(
                pieces[i].at[half], feats.at[g * Y + places[dy]], piece_sem.at[g * Y + dy]
            ).start()

    for tb in range(ZL):
        counts[tb] = 0
    for s in range(SOURCES):

        @pl.loop(0, ZL)
        def _(tb):
            first[tb, s] = counts[tb]

            @pl.loop(0, MOST)
            def _(r):
                block = table[tb, sources[s], r]

                @pl.when(block >= 0)
                def _():
                    slot = tb * cap + counts[tb]
                    pltpu.make_async_copy(
                        queries[s].at[block], picked.at[slot], pick_sem.at[slot]
                    ).start()
                    counts[tb] = counts[tb] + 1

    @pl.loop(0, ZL)
    def _(tb):
        @pl.loop(0, counts[tb])
        def _(p):
            slot = tb * cap + p
            pltpu.make_async_copy(
                queries[0].at[0], picked.at[slot], pick_sem.at[slot]
            ).wait()

    group = 16
    rows, depth = picked.shape[1:]
    cols = Y * feats.shape[1]

    @pl.loop(0, groups)
    def _(g):
        for dy in range(Y):
            pltpu.make_async_copy(
                pieces[0].at[0], feats.at[g * Y], piece_sem.at[g * Y + dy]
            ).wait()
        tb = block_of[g]
        ones = jnp.ones((8, feats.shape[2] - depth), jnp.bfloat16)
        parts = feats[pl.ds(g * Y, Y), :, depth:].reshape(cols, feats.shape[2] - depth)
        weight = lax.dot_general(
            ones, parts, (((1,), (1,)), ((), ())), preferred_element_type=jnp.float32
        )[:1]

        @pl.loop(0, (counts[tb] + group - 1) // group)
        def _(m):
            q = picked[pl.ds(tb * cap + m * group, group)].reshape(group * rows, depth)
            f = feats[pl.ds(g * Y, Y), :, :depth].reshape(cols, depth)
            product = lax.dot_general(
                q, f, (((1,), (1,)), ((), ())), preferred_element_type=jnp.float32
            )
            scaled = (product * weight).astype(jnp.bfloat16)
            scores[g, pl.ds(m * group, group)] = scaled.reshape(group, rows, cols)

        for s in range(SOURCES):
            pltpu.make_async_copy(
                scores.at[g, pl.ds(first[tb, s], MOST)],
                outs[s].at[g],
                out_sem.at[g * SOURCES + s],
            ).start()

    @pl.loop(0, groups * SOURCES)
    def _(i):
        pltpu.make_async_copy(
            scores.at[0, pl.ds(0, MOST)], outs[0].at[0], out_sem.at[i]
        ).wait()


def score(groups, where, table, sources, places, block_of, pieces, ring):
    rows, depth = ring[0].shape[1:]
    piece_rows, wide = pieces[0].shape[1:]
    cols = Y * piece_rows
    cap = SOURCES * MOST
    smem = pl.BlockSpec(memory_space=pltpu.SMEM)
    anywhere = pl.BlockSpec(memory_space=pltpu.HBM)
    return pl.pallas_call(
        functools.partial(score_kernel, groups, where),
        out_shape=[jax.ShapeDtypeStruct((groups, MOST, rows, cols), jnp.bfloat16)] * SOURCES,
        in_specs=[smem] * 4 + [anywhere] * (len(pieces) + len(ring)),
        out_specs=[anywhere] * SOURCES,
        scratch_shapes=[
            pltpu.VMEM((groups * Y, piece_rows, wide), jnp.bfloat16),
            pltpu.VMEM((ZL * cap, rows, depth), jnp.bfloat16),
            pltpu.VMEM((groups, cap + MOST, rows, cols), jnp.bfloat16),
            pltpu.SMEM((ZL,), jnp.int32),
            pltpu.SMEM((ZL, SOURCES), jnp.int32),
            pltpu.SemaphoreType.DMA((groups * Y,)),
            pltpu.SemaphoreType.DMA((ZL * cap,)),
            pltpu.SemaphoreType.DMA((groups * SOURCES,)),
        ],
        cost_estimate=pl.CostEstimate(
            flops=2 * groups * cap * rows * cols * depth,
            bytes_accessed=groups * cols * depth * 2 + (8 << 20),
            transcendentals=0,
        ),
    )(table, sources, places, block_of, *pieces, *ring)


def place_kernel(select, *refs):
    early, late = refs[:SOURCES], refs[SOURCES : 2 * SOURCES]
    out, held, in_sem = refs[2 * SOURCES :]
    copies = []
    for s in range(SOURCES):
        at = 0
        for part, ref in enumerate((early[s], late[s])):
            copies.append(
                pltpu.make_async_copy(
                    ref, held.at[pl.ds(at, ref.shape[0]), s], in_sem.at[part * SOURCES + s]
                )
            )
            at += ref.shape[0]
    for copy in copies:
        copy.start()
    for copy in copies:
        copy.wait()
    cols = held.shape[-1]

    @pl.loop(0, out.shape[0])
    def _(p):
        for h in range(ZH):
            code = select[p * ZH + h]
            out[p, :, h * cols : (h + 1) * cols] = held[
                code // (SOURCES * MOST), code // MOST % SOURCES, code % MOST
            ]


def local(queries, candidates, train_feat, keep_weight):
    blocks, rows, _ = queries.shape
    cands = candidates.shape[1]
    piece_rows = train_feat.shape[1]
    pairs = blocks * cands
    blk, owner = lax.axis_index("blk"), lax.axis_index("owner")
    zh, y = blk // Y, blk % Y
    zl, x, c = owner // (X * C), owner // C % X, owner % C
    z = zh * ZL + zl

    def turned(a, step):
        return permute(a, lambda y, z, x, c: (y, z, (x + step * (1 - 2 * c)) % X, c))

    a1 = turned(queries, 1)
    a2 = turned(queries, -1)
    a3 = turned(a1, 1)
    ring = []
    for i, a in enumerate((queries, a1, a3, a2)):
        ring += [a, swap_core(a)]

    w = keep_weight.reshape(piece_rows, 1)
    high = lax.reduce_precision(w, 8, 7)
    middle = lax.reduce_precision(w - high, 8, 7)
    low = w - high - middle
    lane = jnp.arange(128)[None, :]
    parts = jnp.where(lane == 0, high, jnp.where(lane == 1, middle, jnp.where(lane == 2, low, 0.0)))
    own = jnp.concatenate([train_feat[0], parts.astype(jnp.bfloat16)], axis=1)[None]

    at = {(0, 0): (own, 0)}

    def one(key):
        return at[key][0][at[key][1] : at[key][1] + 1]

    def pair(*keys):
        return jnp.concatenate([one(key) for key in keys])

    def keep(a, *names):
        for half, key in enumerate(names):
            at[key] = (a, half)

    keep(move_y(own, 1), (1, 0))
    keep(move_z(own, 1), (0, 1))
    keep(move_z(own, -1), (0, 7))
    keep(move_z(one((1, 0)), 1), (1, 1))
    keep(move_z(one((1, 0)), -1), (1, 7))
    keep(move_y(one((1, 0)), 1), (2, 0))
    keep(move_y(pair((0, 0), (0, 1), (0, 7)), -1), (3, 0), (3, 1), (3, 7))
    keep(move_y(pair((1, 1), (1, 7)), 1), (2, 1), (2, 7))
    p2 = move_z(pair((0, 1), (1, 1)), 1)
    m2 = move_z(pair((0, 7), (1, 7)), -1)
    keep(p2, (0, 2), (1, 2))
    keep(m2, (0, 6), (1, 6))
    keep(move_z(p2, 1), (0, 3), (1, 3))
    keep(move_z(m2, -1), (0, 5), (1, 5))
    keep(move_y(pair((0, 2), (0, 6)), -1), (3, 2), (3, 6))
    keep(move_y(pair((1, 2), (1, 6)), 1), (2, 2), (2, 6))
    keep(move_z(one((0, 3)), 1), (0, 4))
    keep(move_z(one((1, 5)), -1), (1, 4))
    keep(move_y(one((0, 5)), -1), (3, 5))
    keep(move_y(one((1, 3)), 1), (2, 3))
    keep(move_z(one((3, 2)), 1), (3, 3))
    keep(move_z(one((2, 6)), -1), (2, 5))
    keep(move_y(one((0, 4)), -1), (3, 4))
    keep(move_y(one((1, 4)), 1), (2, 4))
    places = jnp.stack([(y - dy) % Y for dy in range(Y)]).astype(jnp.int32)

    targets = candidates.reshape(pairs)
    named = doubled(targets, c, lambda y, z, x, c: (y, z, x, c ^ 1))
    named = doubled(named, x & 1, lambda y, z, x, c: (y, z, x ^ 1, c))
    named = doubled(named, x >> 1, lambda y, z, x, c: (y, z, x ^ 2, c))
    named = named.reshape(SOURCES, pairs)

    earlier = (jnp.arange(pairs)[:, None] < jnp.arange(pairs)[None, :]).astype(jnp.float32)
    held = jnp.arange(ZL) * (X * C) + x * C + c
    hot = (named[None] == held[:, None, None]).astype(jnp.float32)
    rank = jnp.dot(hot.reshape(-1, pairs), earlier).reshape(hot.shape)
    chosen = hot[:, :, None, :] * (
        rank[:, :, None, :] == jnp.arange(MOST, dtype=jnp.float32)[None, None, :, None]
    )
    block_of = (jnp.arange(pairs) // cands + 1).astype(jnp.float32)
    table = jnp.sum(chosen * block_of, axis=3).astype(jnp.int32) - 1
    sources = jnp.stack(
        [
            (x - dx * (1 - 2 * (c ^ dc))) % X * C + (c ^ dc)
            for dx in range(X)
            for dc in range(C)
        ]
    ).astype(jnp.int32)

    target_hot = (targets[None, :] == jnp.arange(ZL * X * C)[:, None]).astype(jnp.float32)
    my_rank = jnp.sum(jnp.dot(target_hot, earlier) * target_hot, axis=0).astype(jnp.int32)
    from_x, from_c = targets // C % X, targets % C
    from_index = (from_x - x) * (1 - 2 * c) % X * C + (from_c ^ c)
    order = EARLY + LATE
    row_of = jnp.array([order.index(dz) for dz in range(Z)], jnp.int32)
    away = (z - (jnp.arange(ZH)[None, :] * ZL + targets[:, None] // (X * C))) % Z
    row = jnp.sum(
        jnp.where(away[:, :, None] == jnp.arange(Z)[None, None, :], row_of[None, None, :], 0),
        axis=2,
    )
    select = ((row * SOURCES + from_index[:, None]) * MOST + my_rank[:, None]).reshape(-1)

    returned = []
    for steps in (EARLY, LATE):
        block_of = jnp.stack([(z - dz) % ZL for dz in steps]).astype(jnp.int32)
        arrays, where = [], []
        for dz in steps:
            for dy in range(Y):
                a, half = at[dy, dz]
                i = next((i for i, b in enumerate(arrays) if b is a), len(arrays))
                if i == len(arrays):
                    arrays.append(a)
                where.append((i, half))
        scored = score(
            len(steps), tuple(where), table, sources, places, block_of, arrays, ring
        )
        for s in range(SOURCES):
            dx, dc = s // C, s % C
            if s == 0:
                returned.append(scored[0])
            else:
                returned.append(
                    permute(
                        scored[s],
                        lambda y, z, x, c, dx=dx, dc=dc: (
                            y,
                            z,
                            (x - dx * (1 - 2 * (c ^ dc))) % X,
                            c ^ dc,
                        ),
                    )
                )
    out = pl.pallas_call(
        place_kernel,
        out_shape=jax.ShapeDtypeStruct((pairs, rows, Z * Y * piece_rows // ZL), jnp.bfloat16),
        in_specs=[pl.BlockSpec(memory_space=pltpu.SMEM)]
        + [pl.BlockSpec(memory_space=pltpu.VMEM)] * len(returned),
        out_specs=pl.BlockSpec(memory_space=pltpu.VMEM),
        scratch_shapes=[
            pltpu.VMEM((Z, SOURCES, MOST, rows, Y * piece_rows), jnp.bfloat16),
            pltpu.SemaphoreType.DMA((len(returned),)),
        ],
        name="place",
    )(select, *returned)
    return out.reshape(blocks, cands, rows, -1)


def solution(mesh):
    return jax.shard_map(
        local,
        mesh=mesh,
        in_specs=(
            P(("blk", "owner"), None, None),
            P(("blk", "owner"), None),
            P("owner", "blk", None),
            P("owner", "blk"),
        ),
        out_specs=P(("blk", "owner"), None, None, None),
        check_vma=False,
    )
```

```python
import functools

import jax
import jax.numpy as jnp
from jax import lax
from jax.experimental import pallas as pl
from jax.experimental.pallas import tpu as pltpu
from jax.sharding import PartitionSpec as P


ZH, Y, ZL, X, C = 4, 4, 2, 4, 2
Z = ZH * ZL
BOTH = ("blk", "owner")
MOST = 4
SOURCES = X * C


EARLY, LATE = (0, 1, 7, 2, 6), (3, 5, 4)


def flat(y, z, x, c):
    return ((z // ZL) * Y + y) * (ZL * X * C) + (z % ZL) * X * C + x * C + c


def permute(a, to):
    pairs = [
        (flat(y, z, x, c), flat(*to(y, z, x, c)))
        for z in range(Z)
        for y in range(Y)
        for x in range(X)
        for c in range(C)
    ]
    return lax.ppermute(a, BOTH, pairs)


def move_y(a, step):
    return permute(a, lambda y, z, x, c: ((y + step) % Y, z, x, c))


def move_z(a, step):
    return permute(a, lambda y, z, x, c: (y, (z + step) % Z, x, c))


def swap_core(a):
    return permute(a, lambda y, z, x, c: (y, z, x, c ^ 1))


def doubled(a, bit, to):
    other = permute(a, to)
    return jnp.where(bit == 0, jnp.stack([a, other]), jnp.stack([other, a]))


def score_kernel(groups, where, table, sources, places, block_of, *refs):
    held = max(i for i, _ in where) + 1
    pieces, queries = refs[:held], refs[held : held + SOURCES]
    outs = refs[held + SOURCES : held + 2 * SOURCES]
    feats, picked, scores, counts, first, piece_sem, pick_sem, out_sem = refs[
        held + 2 * SOURCES :
    ]
    cap = SOURCES * MOST
    for g in range(groups):
        for dy in range(Y):
            i, half = where[g * Y + dy]
            pltpu.make_async_copy(
                pieces[i].at[half], feats.at[g * Y + places[dy]], piece_sem.at[g * Y + dy]
            ).start()

    for tb in range(ZL):
        counts[tb] = 0
    for s in range(SOURCES):

        @pl.loop(0, ZL)
        def _(tb):
            first[tb, s] = counts[tb]

            @pl.loop(0, MOST)
            def _(r):
                block = table[tb, sources[s], r]

                @pl.when(block >= 0)
                def _():
                    slot = tb * cap + counts[tb]
                    pltpu.make_async_copy(
                        queries[s].at[block], picked.at[slot], pick_sem.at[slot]
                    ).start()
                    counts[tb] = counts[tb] + 1

    @pl.loop(0, ZL)
    def _(tb):
        @pl.loop(0, counts[tb])
        def _(p):
            slot = tb * cap + p
            pltpu.make_async_copy(
                queries[0].at[0], picked.at[slot], pick_sem.at[slot]
            ).wait()

    group = 16
    rows, depth = picked.shape[1:]
    cols = Y * feats.shape[1]

    @pl.loop(0, groups)
    def _(g):
        for dy in range(Y):
            pltpu.make_async_copy(
                pieces[0].at[0], feats.at[g * Y], piece_sem.at[g * Y + dy]
            ).wait()
        tb = block_of[g]
        ones = jnp.ones((8, feats.shape[2] - depth), jnp.bfloat16)
        parts = feats[pl.ds(g * Y, Y), :, depth:].reshape(cols, feats.shape[2] - depth)
        weight = lax.dot_general(
            ones, parts, (((1,), (1,)), ((), ())), preferred_element_type=jnp.float32
        )[:1]

        @pl.loop(0, (counts[tb] + group - 1) // group)
        def _(m):
            q = picked[pl.ds(tb * cap + m * group, group)].reshape(group * rows, depth)
            f = feats[pl.ds(g * Y, Y), :, :depth].reshape(cols, depth)
            product = lax.dot_general(
                q, f, (((1,), (1,)), ((), ())), preferred_element_type=jnp.float32
            )
            scaled = (product * weight).astype(jnp.bfloat16)
            scores[g, pl.ds(m * group, group)] = scaled.reshape(group, rows, cols)

        for s in range(SOURCES):
            pltpu.make_async_copy(
                scores.at[g, pl.ds(first[tb, s], MOST)],
                outs[s].at[g],
                out_sem.at[g * SOURCES + s],
            ).start()

    @pl.loop(0, groups * SOURCES)
    def _(i):
        pltpu.make_async_copy(
            scores.at[0, pl.ds(0, MOST)], outs[0].at[0], out_sem.at[i]
        ).wait()


def score(groups, where, table, sources, places, block_of, pieces, ring):
    rows, depth = ring[0].shape[1:]
    piece_rows, wide = pieces[0].shape[1:]
    cols = Y * piece_rows
    cap = SOURCES * MOST
    smem = pl.BlockSpec(memory_space=pltpu.SMEM)
    anywhere = pl.BlockSpec(memory_space=pltpu.HBM)
    return pl.pallas_call(
        functools.partial(score_kernel, groups, where),
        out_shape=[jax.ShapeDtypeStruct((groups, MOST, rows, cols), jnp.bfloat16)] * SOURCES,
        in_specs=[smem] * 4 + [anywhere] * (len(pieces) + len(ring)),
        out_specs=[anywhere] * SOURCES,
        scratch_shapes=[
            pltpu.VMEM((groups * Y, piece_rows, wide), jnp.bfloat16),
            pltpu.VMEM((ZL * cap, rows, depth), jnp.bfloat16),
            pltpu.VMEM((groups, cap + MOST, rows, cols), jnp.bfloat16),
            pltpu.SMEM((ZL,), jnp.int32),
            pltpu.SMEM((ZL, SOURCES), jnp.int32),
            pltpu.SemaphoreType.DMA((groups * Y,)),
            pltpu.SemaphoreType.DMA((ZL * cap,)),
            pltpu.SemaphoreType.DMA((groups * SOURCES,)),
        ],
        cost_estimate=pl.CostEstimate(
            flops=2 * groups * cap * rows * cols * depth,
            bytes_accessed=groups * cols * depth * 2 + (8 << 20),
            transcendentals=0,
        ),
    )(table, sources, places, block_of, *pieces, *ring)


def place_kernel(select, *refs):
    early, late = refs[:SOURCES], refs[SOURCES : 2 * SOURCES]
    out, held, in_sem = refs[2 * SOURCES :]
    copies = []
    for s in range(SOURCES):
        at = 0
        for part, ref in enumerate((early[s], late[s])):
            copies.append(
                pltpu.make_async_copy(
                    ref, held.at[pl.ds(at, ref.shape[0]), s], in_sem.at[part * SOURCES + s]
                )
            )
            at += ref.shape[0]
    for copy in copies:
        copy.start()
    for copy in copies:
        copy.wait()
    cols = held.shape[-1]

    @pl.loop(0, out.shape[0])
    def _(p):
        for h in range(ZH):
            code = select[p * ZH + h]
            out[p, :, h * cols : (h + 1) * cols] = held[
                code // (SOURCES * MOST), code // MOST % SOURCES, code % MOST
            ]


def local(queries, candidates, train_feat, keep_weight):
    blocks, rows, _ = queries.shape
    cands = candidates.shape[1]
    piece_rows = train_feat.shape[1]
    pairs = blocks * cands
    blk, owner = lax.axis_index("blk"), lax.axis_index("owner")
    zh, y = blk // Y, blk % Y
    zl, x, c = owner // (X * C), owner // C % X, owner % C
    z = zh * ZL + zl

    def turned(a, step):
        return permute(a, lambda y, z, x, c: (y, z, (x + step * (1 - 2 * c)) % X, c))

    a1 = turned(queries, 1)
    a2 = turned(queries, -1)
    a3 = turned(a1, 1)
    ring = []
    for i, a in enumerate((queries, a1, a3, a2)):
        ring += [a, swap_core(a)]

    w = keep_weight.reshape(piece_rows, 1)
    high = lax.reduce_precision(w, 8, 7)
    middle = lax.reduce_precision(w - high, 8, 7)
    low = w - high - middle
    lane = jnp.arange(128)[None, :]
    parts = jnp.where(lane == 0, high, jnp.where(lane == 1, middle, jnp.where(lane == 2, low, 0.0)))
    own = jnp.concatenate([train_feat[0], parts.astype(jnp.bfloat16)], axis=1)[None]

    at = {(0, 0): (own, 0)}

    def one(key):
        return at[key][0][at[key][1] : at[key][1] + 1]

    def pair(*keys):
        return jnp.concatenate([one(key) for key in keys])

    def keep(a, *names):
        for half, key in enumerate(names):
            at[key] = (a, half)

    keep(move_y(own, 1), (1, 0))
    keep(move_z(own, 1), (0, 1))
    keep(move_z(own, -1), (0, 7))
    keep(move_z(one((1, 0)), 1), (1, 1))
    keep(move_z(one((1, 0)), -1), (1, 7))
    keep(move_y(one((1, 0)), 1), (2, 0))
    keep(move_y(pair((0, 0), (0, 1), (0, 7)), -1), (3, 0), (3, 1), (3, 7))
    keep(move_y(pair((1, 1), (1, 7)), 1), (2, 1), (2, 7))
    p2 = move_z(pair((0, 1), (1, 1)), 1)
    m2 = move_z(pair((0, 7), (1, 7)), -1)
    keep(p2, (0, 2), (1, 2))
    keep(m2, (0, 6), (1, 6))
    keep(move_z(p2, 1), (0, 3), (1, 3))
    keep(move_z(m2, -1), (0, 5), (1, 5))
    low_pair = pair((0, 2), (0, 6))
    high_pair = pair((1, 2), (1, 6))
    keep(move_y(low_pair, -1), (3, 2), (3, 6))
    keep(move_y(high_pair, 1), (2, 2), (2, 6))
    keep(move_z(one((0, 3)), 1), (0, 4))
    keep(move_z(one((1, 5)), -1), (1, 4))
    keep(move_y(one((0, 5)), -1), (3, 5))
    keep(move_y(one((1, 3)), 1), (2, 3))
    keep(move_z(one((3, 2)), 1), (3, 3))
    keep(move_z(one((2, 6)), -1), (2, 5))
    keep(move_y(one((0, 4)), -1), (3, 4))
    keep(move_y(one((1, 4)), 1), (2, 4))
    places = jnp.stack([(y - dy) % Y for dy in range(Y)]).astype(jnp.int32)

    targets = candidates.reshape(pairs)
    named = doubled(targets, c, lambda y, z, x, c: (y, z, x, c ^ 1))
    named = doubled(named, x & 1, lambda y, z, x, c: (y, z, x ^ 1, c))
    named = doubled(named, x >> 1, lambda y, z, x, c: (y, z, x ^ 2, c))
    named = named.reshape(SOURCES, pairs)

    earlier = (jnp.arange(pairs)[:, None] < jnp.arange(pairs)[None, :]).astype(jnp.float32)
    held = jnp.arange(ZL) * (X * C) + x * C + c
    hot = (named[None] == held[:, None, None]).astype(jnp.float32)
    rank = jnp.dot(hot.reshape(-1, pairs), earlier).reshape(hot.shape)
    chosen = hot[:, :, None, :] * (
        rank[:, :, None, :] == jnp.arange(MOST, dtype=jnp.float32)[None, None, :, None]
    )
    block_of = (jnp.arange(pairs) // cands + 1).astype(jnp.float32)
    table = jnp.sum(chosen * block_of, axis=3).astype(jnp.int32) - 1
    sources = jnp.stack(
        [
            (x - dx * (1 - 2 * (c ^ dc))) % X * C + (c ^ dc)
            for dx in range(X)
            for dc in range(C)
        ]
    ).astype(jnp.int32)

    target_hot = (targets[None, :] == jnp.arange(ZL * X * C)[:, None]).astype(jnp.float32)
    my_rank = jnp.sum(jnp.dot(target_hot, earlier) * target_hot, axis=0).astype(jnp.int32)
    from_x, from_c = targets // C % X, targets % C
    from_index = (from_x - x) * (1 - 2 * c) % X * C + (from_c ^ c)
    order = EARLY + LATE
    row_of = jnp.array([order.index(dz) for dz in range(Z)], jnp.int32)
    away = (z - (jnp.arange(ZH)[None, :] * ZL + targets[:, None] // (X * C))) % Z
    row = jnp.sum(
        jnp.where(away[:, :, None] == jnp.arange(Z)[None, None, :], row_of[None, None, :], 0),
        axis=2,
    )
    select = ((row * SOURCES + from_index[:, None]) * MOST + my_rank[:, None]).reshape(-1)

    returned = []
    for steps in (EARLY, LATE):
        block_of = jnp.stack([(z - dz) % ZL for dz in steps]).astype(jnp.int32)
        arrays, where = [], []
        for dz in steps:
            for dy in range(Y):
                a, half = at[dy, dz]
                i = next((i for i, b in enumerate(arrays) if b is a), len(arrays))
                if i == len(arrays):
                    arrays.append(a)
                where.append((i, half))
        scored = score(
            len(steps), tuple(where), table, sources, places, block_of, arrays, ring
        )
        for s in range(SOURCES):
            dx, dc = s // C, s % C
            if s == 0:
                returned.append(scored[0])
            else:
                returned.append(
                    permute(
                        scored[s],
                        lambda y, z, x, c, dx=dx, dc=dc: (
                            y,
                            z,
                            (x - dx * (1 - 2 * (c ^ dc))) % X,
                            c ^ dc,
                        ),
                    )
                )
    out = pl.pallas_call(
        place_kernel,
        out_shape=jax.ShapeDtypeStruct((pairs, rows, Z * Y * piece_rows // ZL), jnp.bfloat16),
        in_specs=[pl.BlockSpec(memory_space=pltpu.SMEM)]
        + [pl.BlockSpec(memory_space=pltpu.VMEM)] * len(returned),
        out_specs=pl.BlockSpec(memory_space=pltpu.VMEM),
        scratch_shapes=[
            pltpu.VMEM((Z, SOURCES, MOST, rows, Y * piece_rows), jnp.bfloat16),
            pltpu.SemaphoreType.DMA((len(returned),)),
        ],
        name="place",
    )(select, *returned)
    return out.reshape(blocks, cands, rows, -1)


def solution(mesh):
    return jax.shard_map(
        local,
        mesh=mesh,
        in_specs=(
            P(("blk", "owner"), None, None),
            P(("blk", "owner"), None),
            P("owner", "blk", None),
            P("owner", "blk"),
        ),
        out_specs=P(("blk", "owner"), None, None, None),
        check_vma=False,
    )
```

```python
import functools

import jax
import jax.numpy as jnp
from jax import lax
from jax.experimental import pallas as pl
from jax.experimental.pallas import tpu as pltpu
from jax.sharding import PartitionSpec as P


ZH, Y, ZL, X, C = 4, 4, 2, 4, 2
Z = ZH * ZL
BOTH = ("blk", "owner")
MOST = 4
SOURCES = X * C


EARLY, LATE = (0, 1, 7, 2, 6), (3, 5, 4)


def flat(y, z, x, c):
    return ((z // ZL) * Y + y) * (ZL * X * C) + (z % ZL) * X * C + x * C + c


def permute(a, to):
    pairs = [
        (flat(y, z, x, c), flat(*to(y, z, x, c)))
        for z in range(Z)
        for y in range(Y)
        for x in range(X)
        for c in range(C)
    ]
    return lax.ppermute(a, BOTH, pairs)


def move_y(a, step):
    return permute(a, lambda y, z, x, c: ((y + step) % Y, z, x, c))


def move_z(a, step):
    return permute(a, lambda y, z, x, c: (y, (z + step) % Z, x, c))


def swap_core(a):
    return permute(a, lambda y, z, x, c: (y, z, x, c ^ 1))


def doubled(a, bit, to):
    other = permute(a, to)
    return jnp.where(bit == 0, jnp.stack([a, other]), jnp.stack([other, a]))


def score_kernel(groups, where, info_at, info, *refs):
    held = max(i for i, _ in where) + 1
    pieces, queries = refs[:held], refs[held : held + SOURCES]
    outs = refs[held + SOURCES : held + 2 * SOURCES]
    feats, picked, scores, counts, first, piece_sem, pick_sem, out_sem = refs[
        held + 2 * SOURCES :
    ]
    cap = SOURCES * MOST
    sources_at = ZL * cap
    places_at = sources_at + SOURCES
    for g in range(groups):
        for dy in range(Y):
            i, half = where[g * Y + dy]
            pltpu.make_async_copy(
                pieces[i].at[half], feats.at[g * Y + info[places_at + dy]], piece_sem.at[g * Y + dy]
            ).start()

    for tb in range(ZL):
        counts[tb] = 0
    for s in range(SOURCES):

        @pl.loop(0, ZL)
        def _(tb):
            count = counts[tb]
            first[tb, s] = count
            base = tb * cap + info[sources_at + s] * MOST
            for r in range(MOST):
                block = info[base + r]
                slot = tb * cap + count

                @pl.when(block >= 0)
                def _():
                    pltpu.make_async_copy(
                        queries[s].at[block], picked.at[slot], pick_sem.at[slot]
                    ).start()

                count = count + jnp.where(block >= 0, 1, 0)
            counts[tb] = count

    @pl.loop(0, ZL)
    def _(tb):
        @pl.loop(0, counts[tb])
        def _(p):
            slot = tb * cap + p
            pltpu.make_async_copy(
                queries[0].at[0], picked.at[slot], pick_sem.at[slot]
            ).wait()

    group = 16
    rows, depth = picked.shape[1:]
    cols = Y * feats.shape[1]

    @pl.loop(0, groups)
    def _(g):
        for dy in range(Y):
            pltpu.make_async_copy(
                pieces[0].at[0], feats.at[g * Y], piece_sem.at[g * Y + dy]
            ).wait()
        tb = info[info_at + g]
        ones = jnp.ones((8, feats.shape[2] - depth), jnp.bfloat16)
        parts = feats[pl.ds(g * Y, Y), :, depth:].reshape(cols, feats.shape[2] - depth)
        weight = lax.dot_general(
            ones, parts, (((1,), (1,)), ((), ())), preferred_element_type=jnp.float32
        )[:1]

        @pl.loop(0, (counts[tb] + group - 1) // group)
        def _(m):
            q = picked[pl.ds(tb * cap + m * group, group)].reshape(group * rows, depth)
            f = feats[pl.ds(g * Y, Y), :, :depth].reshape(cols, depth)
            product = lax.dot_general(
                q, f, (((1,), (1,)), ((), ())), preferred_element_type=jnp.float32
            )
            scaled = (product * weight).astype(jnp.bfloat16)
            scores[g, pl.ds(m * group, group)] = scaled.reshape(group, rows, cols)

        for s in range(SOURCES):
            pltpu.make_async_copy(
                scores.at[g, pl.ds(first[tb, s], MOST)],
                outs[s].at[g],
                out_sem.at[g * SOURCES + s],
            ).start()

    @pl.loop(0, groups * SOURCES)
    def _(i):
        pltpu.make_async_copy(
            scores.at[0, pl.ds(0, MOST)], outs[0].at[0], out_sem.at[i]
        ).wait()


def score(groups, where, info_at, info, pieces, ring):
    rows, depth = ring[0].shape[1:]
    piece_rows, wide = pieces[0].shape[1:]
    cols = Y * piece_rows
    cap = SOURCES * MOST
    smem = pl.BlockSpec(memory_space=pltpu.SMEM)
    anywhere = pl.BlockSpec(memory_space=pltpu.HBM)
    return pl.pallas_call(
        functools.partial(score_kernel, groups, where, info_at),
        out_shape=[jax.ShapeDtypeStruct((groups, MOST, rows, cols), jnp.bfloat16)] * SOURCES,
        in_specs=[smem] + [anywhere] * (len(pieces) + len(ring)),
        out_specs=[anywhere] * SOURCES,
        scratch_shapes=[
            pltpu.VMEM((groups * Y, piece_rows, wide), jnp.bfloat16),
            pltpu.VMEM((ZL * cap, rows, depth), jnp.bfloat16),
            pltpu.VMEM((groups, cap + MOST, rows, cols), jnp.bfloat16),
            pltpu.SMEM((ZL,), jnp.int32),
            pltpu.SMEM((ZL, SOURCES), jnp.int32),
            pltpu.SemaphoreType.DMA((groups * Y,)),
            pltpu.SemaphoreType.DMA((ZL * cap,)),
            pltpu.SemaphoreType.DMA((groups * SOURCES,)),
        ],
        cost_estimate=pl.CostEstimate(
            flops=2 * groups * cap * rows * cols * depth,
            bytes_accessed=groups * cols * depth * 2 + (8 << 20),
            transcendentals=0,
        ),
    )(info, *pieces, *ring)


def place_kernel(select, *refs):
    early, late = refs[:SOURCES], refs[SOURCES : 2 * SOURCES]
    out, held, in_sem = refs[2 * SOURCES :]
    copies = []
    for s in range(SOURCES):
        at = 0
        for part, ref in enumerate((early[s], late[s])):
            copies.append(
                pltpu.make_async_copy(
                    ref, held.at[pl.ds(at, ref.shape[0]), s], in_sem.at[part * SOURCES + s]
                )
            )
            at += ref.shape[0]
    for copy in copies:
        copy.start()
    for copy in copies:
        copy.wait()
    cols = held.shape[-1]

    @pl.loop(0, out.shape[0])
    def _(p):
        for h in range(ZH):
            code = select[p * ZH + h]
            out[p, :, h * cols : (h + 1) * cols] = held[
                code // (SOURCES * MOST), code // MOST % SOURCES, code % MOST
            ]


def local(queries, candidates, train_feat, keep_weight):
    blocks, rows, _ = queries.shape
    cands = candidates.shape[1]
    piece_rows = train_feat.shape[1]
    pairs = blocks * cands
    blk, owner = lax.axis_index("blk"), lax.axis_index("owner")
    zh, y = blk // Y, blk % Y
    zl, x, c = owner // (X * C), owner // C % X, owner % C
    z = zh * ZL + zl

    def turned(a, step):
        return permute(a, lambda y, z, x, c: (y, z, (x + step * (1 - 2 * c)) % X, c))

    a1 = turned(queries, 1)
    a2 = turned(queries, -1)
    a3 = turned(a1, 1)
    ring = []
    for i, a in enumerate((queries, a1, a3, a2)):
        ring += [a, swap_core(a)]

    w = keep_weight.reshape(piece_rows, 1)
    high = lax.reduce_precision(w, 8, 7)
    middle = lax.reduce_precision(w - high, 8, 7)
    low = w - high - middle
    lane = jnp.arange(128)[None, :]
    parts = jnp.where(lane == 0, high, jnp.where(lane == 1, middle, jnp.where(lane == 2, low, 0.0)))
    own = jnp.concatenate([train_feat[0], parts.astype(jnp.bfloat16)], axis=1)[None]

    at = {(0, 0): (own, 0)}

    def one(key):
        return at[key][0][at[key][1] : at[key][1] + 1]

    def pair(*keys):
        return jnp.concatenate([one(key) for key in keys])

    def keep(a, *names):
        for half, key in enumerate(names):
            at[key] = (a, half)

    keep(move_y(own, 1), (1, 0))
    keep(move_z(own, 1), (0, 1))
    keep(move_z(own, -1), (0, 7))
    keep(move_z(one((1, 0)), 1), (1, 1))
    keep(move_z(one((1, 0)), -1), (1, 7))
    keep(move_y(one((1, 0)), 1), (2, 0))
    keep(move_y(pair((0, 0), (0, 1), (0, 7)), -1), (3, 0), (3, 1), (3, 7))
    keep(move_y(pair((1, 1), (1, 7)), 1), (2, 1), (2, 7))
    p2 = move_z(pair((0, 1), (1, 1)), 1)
    m2 = move_z(pair((0, 7), (1, 7)), -1)
    keep(p2, (0, 2), (1, 2))
    keep(m2, (0, 6), (1, 6))
    keep(move_z(p2, 1), (0, 3), (1, 3))
    keep(move_z(m2, -1), (0, 5), (1, 5))
    low_pair = pair((0, 2), (0, 6))
    high_pair = pair((1, 2), (1, 6))
    keep(move_y(low_pair, -1), (3, 2), (3, 6))
    keep(move_y(high_pair, 1), (2, 2), (2, 6))
    keep(move_z(one((0, 3)), 1), (0, 4))
    keep(move_z(one((1, 5)), -1), (1, 4))
    keep(move_y(one((0, 5)), -1), (3, 5))
    keep(move_y(one((1, 3)), 1), (2, 3))
    keep(move_z(one((3, 2)), 1), (3, 3))
    keep(move_z(one((2, 6)), -1), (2, 5))
    keep(move_y(one((0, 4)), -1), (3, 4))
    keep(move_y(one((1, 4)), 1), (2, 4))
    targets = candidates.reshape(pairs)
    named = doubled(targets, c, lambda y, z, x, c: (y, z, x, c ^ 1))
    named = doubled(named, x & 1, lambda y, z, x, c: (y, z, x ^ 1, c))
    named = doubled(named, x >> 1, lambda y, z, x, c: (y, z, x ^ 2, c))
    named = named.reshape(SOURCES, pairs)

    earlier = (jnp.arange(pairs)[:, None] < jnp.arange(pairs)[None, :]).astype(jnp.float32)
    held = jnp.arange(ZL) * (X * C) + x * C + c
    hot = (named[None] == held[:, None, None]).astype(jnp.float32)
    rank = jnp.dot(hot.reshape(-1, pairs), earlier).reshape(hot.shape)
    chosen = hot[:, :, None, :] * (
        rank[:, :, None, :] == jnp.arange(MOST, dtype=jnp.float32)[None, None, :, None]
    )
    block_of = (jnp.arange(pairs) // cands + 1).astype(jnp.float32)
    table = jnp.sum(chosen * block_of, axis=3).astype(jnp.int32) - 1
    sources = jnp.stack(
        [
            (x - dx * (1 - 2 * (c ^ dc))) % X * C + (c ^ dc)
            for dx in range(X)
            for dc in range(C)
        ]
    ).astype(jnp.int32)

    target_hot = (targets[None, :] == jnp.arange(ZL * X * C)[:, None]).astype(jnp.float32)
    my_rank = jnp.sum(jnp.dot(target_hot, earlier) * target_hot, axis=0).astype(jnp.int32)
    from_x, from_c = targets // C % X, targets % C
    from_index = (from_x - x) * (1 - 2 * c) % X * C + (from_c ^ c)
    order = EARLY + LATE
    row_of = jnp.array([order.index(dz) for dz in range(Z)], jnp.int32)
    away = (z - (jnp.arange(ZH)[None, :] * ZL + targets[:, None] // (X * C))) % Z
    row = jnp.sum(
        jnp.where(away[:, :, None] == jnp.arange(Z)[None, None, :], row_of[None, None, :], 0),
        axis=2,
    )
    select = ((row * SOURCES + from_index[:, None]) * MOST + my_rank[:, None]).reshape(-1)
    places = jnp.stack([(y - dy) % Y for dy in range(Y)]).astype(jnp.int32)
    block_of = jnp.stack([(z - dz) % ZL for dz in order]).astype(jnp.int32)
    info = jnp.concatenate([table.reshape(-1), sources, places, block_of])

    info_at = table.size + SOURCES + Y
    returned = []
    for steps in (EARLY, LATE):
        arrays, where = [], []
        for dz in steps:
            for dy in range(Y):
                a, half = at[dy, dz]
                i = next((i for i, b in enumerate(arrays) if b is a), len(arrays))
                if i == len(arrays):
                    arrays.append(a)
                where.append((i, half))
        scored = score(len(steps), tuple(where), info_at, info, arrays, ring)
        info_at += len(steps)
        for s in range(SOURCES):
            dx, dc = s // C, s % C
            if s == 0:
                returned.append(scored[0])
            else:
                returned.append(
                    permute(
                        scored[s],
                        lambda y, z, x, c, dx=dx, dc=dc: (
                            y,
                            z,
                            (x - dx * (1 - 2 * (c ^ dc))) % X,
                            c ^ dc,
                        ),
                    )
                )
    out = pl.pallas_call(
        place_kernel,
        out_shape=jax.ShapeDtypeStruct((pairs, rows, Z * Y * piece_rows // ZL), jnp.bfloat16),
        in_specs=[pl.BlockSpec(memory_space=pltpu.SMEM)]
        + [pl.BlockSpec(memory_space=pltpu.VMEM)] * len(returned),
        out_specs=pl.BlockSpec(memory_space=pltpu.VMEM),
        scratch_shapes=[
            pltpu.VMEM((Z, SOURCES, MOST, rows, Y * piece_rows), jnp.bfloat16),
            pltpu.SemaphoreType.DMA((len(returned),)),
        ],
        name="place",
    )(select, *returned)
    return out.reshape(blocks, cands, rows, -1)


def solution(mesh):
    return jax.shard_map(
        local,
        mesh=mesh,
        in_specs=(
            P(("blk", "owner"), None, None),
            P(("blk", "owner"), None),
            P("owner", "blk", None),
            P("owner", "blk"),
        ),
        out_specs=P(("blk", "owner"), None, None, None),
        check_vma=False,
    )
```

```python
import functools

import jax
import jax.numpy as jnp
from jax import lax
from jax.experimental import pallas as pl
from jax.experimental.pallas import tpu as pltpu
from jax.sharding import PartitionSpec as P


ZH, Y, ZL, X, C = 4, 4, 2, 4, 2
Z = ZH * ZL
BOTH = ("blk", "owner")
MOST = 4
SOURCES = X * C


EARLY, LATE = (0, 1, 7, 2, 6), (3, 5, 4)


def flat(y, z, x, c):
    return ((z // ZL) * Y + y) * (ZL * X * C) + (z % ZL) * X * C + x * C + c


def permute(a, to):
    pairs = [
        (flat(y, z, x, c), flat(*to(y, z, x, c)))
        for z in range(Z)
        for y in range(Y)
        for x in range(X)
        for c in range(C)
    ]
    return lax.ppermute(a, BOTH, pairs)


def move_y(a, step):
    return permute(a, lambda y, z, x, c: ((y + step) % Y, z, x, c))


def move_z(a, step):
    return permute(a, lambda y, z, x, c: (y, (z + step) % Z, x, c))


def swap_core(a):
    return permute(a, lambda y, z, x, c: (y, z, x, c ^ 1))


def doubled(a, bit, to):
    other = permute(a, to)
    return jnp.where(bit == 0, jnp.stack([a, other]), jnp.stack([other, a]))


def score_kernel(groups, where, info_at, info, *refs):
    held = max(i for i, _ in where) + 1
    pieces, queries = refs[:held], refs[held : held + SOURCES]
    outs = refs[held + SOURCES : held + 2 * SOURCES]
    feats, picked, scores, counts, first, piece_sem, pick_sem, out_sem = refs[
        held + 2 * SOURCES :
    ]
    cap = SOURCES * MOST
    sources_at = ZL * cap
    places_at = sources_at + SOURCES
    for g in range(groups):
        for dy in range(Y):
            i, half = where[g * Y + dy]
            pltpu.make_async_copy(
                pieces[i].at[half], feats.at[g * Y + info[places_at + dy]], piece_sem.at[g * Y + dy]
            ).start()

    for tb in range(ZL):
        counts[tb] = 0
    for s in range(SOURCES):

        @pl.loop(0, ZL)
        def _(tb):
            count = counts[tb]
            first[tb, s] = count
            base = tb * cap + info[sources_at + s] * MOST
            for r in range(MOST):
                block = info[base + r]
                slot = tb * cap + count

                @pl.when(block >= 0)
                def _():
                    pltpu.make_async_copy(
                        queries[s].at[block], picked.at[slot], pick_sem.at[slot]
                    ).start()

                count = count + jnp.where(block >= 0, 1, 0)
            counts[tb] = count

    @pl.loop(0, ZL)
    def _(tb):
        @pl.loop(0, counts[tb])
        def _(p):
            slot = tb * cap + p
            pltpu.make_async_copy(
                queries[0].at[0], picked.at[slot], pick_sem.at[slot]
            ).wait()

    group = 16
    rows, depth = picked.shape[1:]
    cols = Y * feats.shape[1]

    @pl.loop(0, groups)
    def _(g):
        for dy in range(Y):
            pltpu.make_async_copy(
                pieces[0].at[0], feats.at[g * Y], piece_sem.at[g * Y + dy]
            ).wait()
        tb = info[info_at + g]
        ones = jnp.ones((8, feats.shape[2] - depth), jnp.bfloat16)
        parts = feats[pl.ds(g * Y, Y), :, depth:].reshape(cols, feats.shape[2] - depth)
        weight = lax.dot_general(
            ones, parts, (((1,), (1,)), ((), ())), preferred_element_type=jnp.float32
        )[:1]

        @pl.loop(0, (counts[tb] + group - 1) // group)
        def _(m):
            q = picked[pl.ds(tb * cap + m * group, group)].reshape(group * rows, depth)
            f = feats[pl.ds(g * Y, Y), :, :depth].reshape(cols, depth)
            product = lax.dot_general(
                q, f, (((1,), (1,)), ((), ())), preferred_element_type=jnp.float32
            )
            scaled = (product * weight).astype(jnp.bfloat16)
            scores[g, pl.ds(m * group, group)] = scaled.reshape(group, rows, cols)

        for s in range(SOURCES):
            pltpu.make_async_copy(
                scores.at[g, pl.ds(first[tb, s], MOST)],
                outs[s].at[g],
                out_sem.at[g * SOURCES + s],
            ).start()

    @pl.loop(0, groups * SOURCES)
    def _(i):
        pltpu.make_async_copy(
            scores.at[0, pl.ds(0, MOST)], outs[0].at[0], out_sem.at[i]
        ).wait()


def score(groups, where, info_at, info, pieces, ring):
    rows, depth = ring[0].shape[1:]
    piece_rows, wide = pieces[0].shape[1:]
    cols = Y * piece_rows
    cap = SOURCES * MOST
    smem = pl.BlockSpec(memory_space=pltpu.SMEM)
    anywhere = pl.BlockSpec(memory_space=pltpu.HBM)
    return pl.pallas_call(
        functools.partial(score_kernel, groups, where, info_at),
        out_shape=[jax.ShapeDtypeStruct((groups, MOST, rows, cols), jnp.bfloat16)] * SOURCES,
        in_specs=[smem] + [anywhere] * (len(pieces) + len(ring)),
        out_specs=[anywhere] * SOURCES,
        scratch_shapes=[
            pltpu.VMEM((groups * Y, piece_rows, wide), jnp.bfloat16),
            pltpu.VMEM((ZL * cap, rows, depth), jnp.bfloat16),
            pltpu.VMEM((groups, cap + MOST, rows, cols), jnp.bfloat16),
            pltpu.SMEM((ZL,), jnp.int32),
            pltpu.SMEM((ZL, SOURCES), jnp.int32),
            pltpu.SemaphoreType.DMA((groups * Y,)),
            pltpu.SemaphoreType.DMA((ZL * cap,)),
            pltpu.SemaphoreType.DMA((groups * SOURCES,)),
        ],
        cost_estimate=pl.CostEstimate(
            flops=2 * groups * cap * rows * cols * depth,
            bytes_accessed=groups * cols * depth * 2 + (8 << 20),
            transcendentals=0,
        ),
    )(info, *pieces, *ring)


def place_kernel(select, *refs):
    early, late = refs[:SOURCES], refs[SOURCES : 2 * SOURCES]
    out, held, in_sem = refs[2 * SOURCES :]
    copies = []
    for s in range(SOURCES):
        at = 0
        for part, ref in enumerate((early[s], late[s])):
            copies.append(
                pltpu.make_async_copy(
                    ref, held.at[pl.ds(at, ref.shape[0]), s], in_sem.at[part * SOURCES + s]
                )
            )
            at += ref.shape[0]
    for copy in copies:
        copy.start()
    for copy in copies:
        copy.wait()
    cols = held.shape[-1]

    @pl.loop(0, out.shape[0])
    def _(p):
        for h in range(ZH):
            code = select[p * ZH + h]
            out[p, :, h * cols : (h + 1) * cols] = held[
                code // (SOURCES * MOST), code // MOST % SOURCES, code % MOST
            ]


def local(queries, candidates, train_feat, keep_weight):
    blocks, rows, _ = queries.shape
    cands = candidates.shape[1]
    piece_rows = train_feat.shape[1]
    pairs = blocks * cands
    blk, owner = lax.axis_index("blk"), lax.axis_index("owner")
    zh, y = blk // Y, blk % Y
    zl, x, c = owner // (X * C), owner // C % X, owner % C
    z = zh * ZL + zl

    def turned(a, step):
        return permute(a, lambda y, z, x, c: (y, z, (x + step * (1 - 2 * c)) % X, c))

    a1 = turned(queries, 1)
    a2 = turned(queries, -1)
    a3 = turned(a1, 1)
    ring = []
    for i, a in enumerate((queries, a1, a3, a2)):
        ring += [a, swap_core(a)]

    w = keep_weight.reshape(piece_rows, 1)
    high = lax.reduce_precision(w, 8, 7)
    middle = lax.reduce_precision(w - high, 8, 7)
    low = w - high - middle
    lane = jnp.arange(128)[None, :]
    parts = jnp.where(lane == 0, high, jnp.where(lane == 1, middle, jnp.where(lane == 2, low, 0.0)))
    own = jnp.concatenate([train_feat[0], parts.astype(jnp.bfloat16)], axis=1)[None]

    at = {(0, 0): (own, 0)}

    def one(key):
        return at[key][0][at[key][1] : at[key][1] + 1]

    def pair(*keys):
        return jnp.concatenate([one(key) for key in keys])

    def keep(a, *names):
        for half, key in enumerate(names):
            at[key] = (a, half)

    keep(move_y(own, 1), (1, 0))
    keep(move_z(own, 1), (0, 1))
    keep(move_z(own, -1), (0, 7))
    keep(move_z(one((1, 0)), 1), (1, 1))
    keep(move_z(one((1, 0)), -1), (1, 7))
    keep(move_y(one((1, 0)), 1), (2, 0))
    keep(move_y(pair((0, 0), (0, 1), (0, 7)), -1), (3, 0), (3, 1), (3, 7))
    keep(move_y(pair((1, 1), (1, 7)), 1), (2, 1), (2, 7))
    for dy in (0, 1):
        keep(move_z(one((dy, 1)), 1), (dy, 2))
        keep(move_z(one((dy, 7)), -1), (dy, 6))
    keep(move_y(pair((0, 2), (0, 6)), -1), (3, 2), (3, 6))
    keep(move_y(pair((1, 2), (1, 6)), 1), (2, 2), (2, 6))
    keep(move_z(pair((0, 2), (1, 2)), 1), (0, 3), (1, 3))
    keep(move_z(pair((0, 6), (1, 6)), -1), (0, 5), (1, 5))
    keep(move_z(one((0, 3)), 1), (0, 4))
    keep(move_z(one((1, 5)), -1), (1, 4))
    low_pair = pair((0, 3), (0, 5))
    high_pair = pair((1, 3), (1, 5))
    keep(move_y(low_pair, -1), (3, 3), (3, 5))
    keep(move_y(high_pair, 1), (2, 3), (2, 5))
    keep(move_y(one((0, 4)), -1), (3, 4))
    keep(move_y(one((1, 4)), 1), (2, 4))

    targets = candidates.reshape(pairs)
    named = doubled(targets, c, lambda y, z, x, c: (y, z, x, c ^ 1))
    named = doubled(named, x & 1, lambda y, z, x, c: (y, z, x ^ 1, c))
    named = doubled(named, x >> 1, lambda y, z, x, c: (y, z, x ^ 2, c))
    named = named.reshape(SOURCES, pairs)

    earlier = (jnp.arange(pairs)[:, None] < jnp.arange(pairs)[None, :]).astype(jnp.float32)
    held = jnp.arange(ZL) * (X * C) + x * C + c
    hot = (named[None] == held[:, None, None]).astype(jnp.float32)
    rank = jnp.dot(hot.reshape(-1, pairs), earlier).reshape(hot.shape)
    chosen = hot[:, :, None, :] * (
        rank[:, :, None, :] == jnp.arange(MOST, dtype=jnp.float32)[None, None, :, None]
    )
    block_of = (jnp.arange(pairs) // cands + 1).astype(jnp.float32)
    table = jnp.sum(chosen * block_of, axis=3).astype(jnp.int32) - 1
    sources = jnp.stack(
        [
            (x - dx * (1 - 2 * (c ^ dc))) % X * C + (c ^ dc)
            for dx in range(X)
            for dc in range(C)
        ]
    ).astype(jnp.int32)

    target_hot = (targets[None, :] == jnp.arange(ZL * X * C)[:, None]).astype(jnp.float32)
    my_rank = jnp.sum(jnp.dot(target_hot, earlier) * target_hot, axis=0).astype(jnp.int32)
    from_x, from_c = targets // C % X, targets % C
    from_index = (from_x - x) * (1 - 2 * c) % X * C + (from_c ^ c)
    order = EARLY + LATE
    row_of = jnp.array([order.index(dz) for dz in range(Z)], jnp.int32)
    away = (z - (jnp.arange(ZH)[None, :] * ZL + targets[:, None] // (X * C))) % Z
    row = jnp.sum(
        jnp.where(away[:, :, None] == jnp.arange(Z)[None, None, :], row_of[None, None, :], 0),
        axis=2,
    )
    select = ((row * SOURCES + from_index[:, None]) * MOST + my_rank[:, None]).reshape(-1)
    places = jnp.stack([(y - dy) % Y for dy in range(Y)]).astype(jnp.int32)
    block_of = jnp.stack([(z - dz) % ZL for dz in order]).astype(jnp.int32)
    info = jnp.concatenate([table.reshape(-1), sources, places, block_of])

    info_at = table.size + SOURCES + Y
    returned = []
    for steps in (EARLY, LATE):
        arrays, where = [], []
        for dz in steps:
            for dy in range(Y):
                a, half = at[dy, dz]
                i = next((i for i, b in enumerate(arrays) if b is a), len(arrays))
                if i == len(arrays):
                    arrays.append(a)
                where.append((i, half))
        scored = score(len(steps), tuple(where), info_at, info, arrays, ring)
        info_at += len(steps)
        for s in range(SOURCES):
            dx, dc = s // C, s % C
            if s == 0:
                returned.append(scored[0])
            else:
                returned.append(
                    permute(
                        scored[s],
                        lambda y, z, x, c, dx=dx, dc=dc: (
                            y,
                            z,
                            (x - dx * (1 - 2 * (c ^ dc))) % X,
                            c ^ dc,
                        ),
                    )
                )
    out = pl.pallas_call(
        place_kernel,
        out_shape=jax.ShapeDtypeStruct((pairs, rows, Z * Y * piece_rows // ZL), jnp.bfloat16),
        in_specs=[pl.BlockSpec(memory_space=pltpu.SMEM)]
        + [pl.BlockSpec(memory_space=pltpu.VMEM)] * len(returned),
        out_specs=pl.BlockSpec(memory_space=pltpu.VMEM),
        scratch_shapes=[
            pltpu.VMEM((Z, SOURCES, MOST, rows, Y * piece_rows), jnp.bfloat16),
            pltpu.SemaphoreType.DMA((len(returned),)),
        ],
        name="place",
    )(select, *returned)
    return out.reshape(blocks, cands, rows, -1)


def solution(mesh):
    return jax.shard_map(
        local,
        mesh=mesh,
        in_specs=(
            P(("blk", "owner"), None, None),
            P(("blk", "owner"), None),
            P("owner", "blk", None),
            P("owner", "blk"),
        ),
        out_specs=P(("blk", "owner"), None, None, None),
        check_vma=False,
    )
```
